256 devices in a mesh: gx: 8 (over z_lo, x), gy: 32 (over z_hi, y, core).
Axes of the slice: x: 4, y: 4, z: 8 (z_hi: 4, z_lo: 2; z = z_hi * 2 + z_lo), core: 2. Of those that a mesh axis runs over, the one named last changes fastest.
Arguments:
- vectors: bfloat16 [65536, 32, 128], P(('gx', 'gy')), may hold values from -6 to 6
- coupling_table: bfloat16 [8, 16, 128, 128], replicated, may hold values from -0.375 to 0.375
- factor_index: int32 [65536, 8, 2], P(('gx', 'gy')), may hold values from 0 to 15
- level_order: int32 [8], replicated, may hold values from 0 to 7, each once
Outputs:
- applied: bfloat16 [65536, 32, 128], P(('gx', 'gy'))
The draws below stay inside these ranges and needn't reach their ends.
Inputs may be any that keep to these rules, and one draw needn't show every extreme that they name: `factor_index`: table entries of the coupling matrices. `level_order`: each level slot appears once.
All inputs are finite; a program needn't handle non-finite values.
Results may differ from the reference program's by a relative error of at most 0.0086.
Values may be sent and summed in bfloat16 or wider, within the bound.
A program may use at most 64 MiB of HBM per device.

```python
import jax
import jax.numpy as jnp
from jax import lax

R = 128
NRHS = 32
NTAB = 16
BLK_DEV = 256
BLOCKS = 65536
LEVELS = 8


def place_ends(array, own_key, smallest, largest):
    longest = array.shape.index(max(array.shape))
    spots = []
    for shift in (0, 1):
        where = [jax.random.randint(jax.random.fold_in(own_key, axis), (), 0, length) for axis, length in enumerate(array.shape)]
        where[longest] = (where[longest] + shift) % array.shape[longest]
        spots.append(tuple(where))
    return array.at[spots[0]].set(smallest).at[spots[1]].set(largest)


def shard_levels(own_key, extent, shards, low, top_value):
    gain = 1.0
    for dim, shards_of in shards:
        draws = jax.random.uniform(jax.random.fold_in(jax.random.fold_in(own_key, 6), dim), (shards_of,), jnp.float32, low / len(shards), top_value / len(shards))
        gain = gain * jnp.repeat(jnp.exp(draws), extent[dim] // shards_of).reshape((-1,) + (1,) * (len(extent) - 1 - dim))
    return gain


def normal_values(key, shape, width, reach, pieces=(), held_as=jnp.bfloat16):
    factor_of = shard_levels(key, shape, pieces, -0.22, 0.18) if pieces else 1.0
    drawn = jax.random.normal(key, shape, jnp.float32) * width * factor_of
    return jnp.minimum(jnp.maximum(drawn, -reach), reach).astype(held_as)


def setup_inputs(seed: int = 0) -> dict:
    keys = jax.random.split(jax.random.key(seed), 5)
    return {
        "vectors": normal_values(keys[0], (BLOCKS, NRHS, R), 1.0, 6.0, ((0, 256),)),
        "coupling_table": normal_values(keys[1], (LEVELS, NTAB, R, R), (2 * R) ** -0.5, 0.375),
        "factor_index": place_ends(jax.random.randint(keys[2], (BLOCKS, LEVELS, 2), 0, NTAB), jax.random.fold_in(keys[2], 1), 0, NTAB - 1).astype(jnp.int32),
        "level_order": jax.random.permutation(keys[3], LEVELS).astype(jnp.int32),
    }


def reference(vectors, coupling_table, factor_index, level_order):
    field = vectors
    block_ids = jnp.arange(BLOCKS, dtype=jnp.int32)
    groups = BLOCKS // BLK_DEV
    for position in range(LEVELS):
        level_slot = level_order[position]
        level_table = lax.dynamic_index_in_dim(coupling_table, level_slot, 0, keepdims=False).astype(jnp.float32)
        chosen = lax.dynamic_index_in_dim(factor_index, level_slot, 1, keepdims=False)
        partner = jnp.take(field, block_ids ^ (BLK_DEV << position), axis=0)

        def one_group(operands):
            own_blocks, other_blocks, selected = operands
            first = level_table[selected[:, 0]]
            second = level_table[selected[:, 1]]
            local_part = jnp.einsum("bnj,bij->bni", own_blocks.astype(jnp.float32), first)
            remote_part = jnp.einsum("bnj,bij->bni", other_blocks.astype(jnp.float32), second)
            return (local_part + remote_part).astype(jnp.bfloat16)

        field = lax.map(one_group, (field.reshape(groups, BLK_DEV, NRHS, R),
                                    partner.reshape(groups, BLK_DEV, NRHS, R),
                                    chosen.reshape(groups, BLK_DEV, 2))).reshape(BLOCKS, NRHS, R)
    return field
```

```python
import functools

import jax
import jax.numpy as jnp
from jax import lax
from jax.experimental import pallas as pl
from jax.experimental.pallas import tpu as pltpu
from jax.sharding import PartitionSpec as P

UNROLL = 4


def levels_kernel(levels, order_ref, index_ref, field_ref, table_ref, out_ref):
    blocks, _, rank = field_ref.shape
    out_ref[...] = field_ref[...]
    for level in range(levels):
        slot = order_ref[level]

        def step(i, carry, level=level, slot=slot):
            done = []
            for u in range(UNROLL):
                t = i * UNROLL + u
                g = ((t >> level) << (level + 1)) | (t & ((1 << level) - 1))
                p = g | (1 << level)
                at_g, at_p = (g * levels + slot) * 2, (p * levels + slot) * 2
                from_g = jnp.concatenate(
                    [table_ref[slot, index_ref[at_g]], table_ref[slot, index_ref[at_p + 1]]], axis=1
                )
                from_p = jnp.concatenate(
                    [table_ref[slot, index_ref[at_g + 1]], table_ref[slot, index_ref[at_p]]], axis=1
                )
                both = jnp.dot(
                    jnp.concatenate([out_ref[g], out_ref[p]], axis=1),
                    jnp.concatenate([from_g, from_p], axis=0),
                    preferred_element_type=jnp.float32,
                ).astype(jnp.bfloat16)
                done.append((g, p, both))
            for g, p, both in done:
                out_ref[g] = both[:, :rank]
                out_ref[p] = both[:, rank:]
            return carry

        lax.fori_loop(0, blocks // 2 // UNROLL, step, 0)


def body(vectors, coupling_table, factor_index, level_order):
    axes = ("gx", "gy")
    blocks, levels = factor_index.shape[:2]
    field = lax.all_to_all(vectors, axes, 0, 0, tiled=True)
    index = lax.all_to_all(factor_index.reshape(blocks, levels * 2), axes, 0, 0, tiled=True)
    smem, vmem = pl.BlockSpec(memory_space=pltpu.SMEM), pl.BlockSpec(memory_space=pltpu.VMEM)
    field = pl.pallas_call(
        functools.partial(levels_kernel, levels),
        out_shape=jax.ShapeDtypeStruct(field.shape, field.dtype),
        in_specs=[smem, smem, vmem, vmem],
        out_specs=vmem,
        compiler_params=pltpu.CompilerParams(vmem_limit_bytes=40 << 20),
    )(level_order, index.reshape(-1), field, jnp.swapaxes(coupling_table, 2, 3))
    return lax.all_to_all(field, axes, 0, 0, tiled=True)


def solution(mesh):
    placed = (P(("gx", "gy"), None, None), P(), P(("gx", "gy"), None, None), P())
    return jax.shard_map(
        body, mesh=mesh, in_specs=placed, out_specs=P(("gx", "gy"), None, None), check_vma=False
    )
```

```python
import jax
import jax.numpy as jnp
from jax import lax
from jax.experimental import pallas as pl
from jax.experimental.pallas import tpu as pltpu
from jax.sharding import PartitionSpec as P

MESH = pl.DeviceIdType.MESH
HIGH, MIDDLE = 8, 32
DEVICES = HIGH * MIDDLE
BATCH = 4


def rotated(coordinate, step):
    z, y, core = coordinate // 8, lax.rem(coordinate // 2, 4), lax.rem(coordinate, 2)
    return (
        lax.rem(z + lax.rem(step, 4), 4) * 8
        + lax.rem(y + lax.rem(step // 4, 4), 4) * 2
        + lax.rem(core + step // 16, 2)
    )


def kernel(
    order, index, vectors, table, out,
    field, raw, flat, near, far, chosen,
    table_sem, near_send, near_recv, far_send, far_recv, chosen_sem,
    out_send, out_recv, field_send, field_recv,
):
    gx, gy = lax.axis_index("gx"), lax.axis_index("gy")
    mine = gy * HIGH + gx
    here = gx * MIDDLE + gy

    table_copy = pltpu.make_async_copy(table, raw, table_sem)
    table_copy.start()

    barrier = pltpu.get_barrier_semaphore()

    def greet(i, carry):
        to = (lax.rem(gx + i // MIDDLE, HIGH), lax.rem(gy + lax.rem(i, MIDDLE), MIDDLE))
        pl.semaphore_signal(barrier, inc=1, device_id=to, device_id_type=MESH)
        return carry

    lax.fori_loop(1, DEVICES, greet, 0)
    pl.semaphore_wait(barrier, DEVICES - 1)

    def send_index(r, carry):
        to = rotated(gy, r)
        pltpu.make_async_remote_copy(
            index.at[to], near.at[gy], near_send, near_recv, device_id=(gx, to), device_id_type=MESH
        ).start()
        return carry

    def send_group(s):
        to_x = lax.rem(gx + s, HIGH)

        def send(r, carry):
            to_y = rotated(gy, r)
            pltpu.make_async_remote_copy(
                vectors.at[to_y * HIGH + to_x], field.at[here], field_send, field_recv.at[s],
                device_id=(to_x, to_y), device_id_type=MESH,
            ).start()
            return carry

        return send

    own_index = pltpu.make_async_copy(index.at[gy], near.at[gy], near_recv)
    own_index.start()
    lax.fori_loop(1, MIDDLE, send_index, 0)
    pltpu.make_async_copy(vectors.at[mine], field.at[here], field_recv.at[0]).start()
    lax.fori_loop(1, MIDDLE, send_group(0), 0)
    lax.fori_loop(0, MIDDLE, send_group(1), 0)
    pltpu.make_async_copy(index, near, near_recv).wait()

    def send_far(s, carry):
        to = lax.rem(gx + s, HIGH)
        pltpu.make_async_remote_copy(
            near, far.at[gx], far_send, far_recv, device_id=(to, gy), device_id_type=MESH
        ).start()
        return carry

    lax.fori_loop(1, HIGH, send_far, 0)
    pltpu.make_async_copy(near, far.at[gx], far_recv).start()

    def send_rest(s, carry):
        lax.fori_loop(0, MIDDLE, send_group(s), 0)
        return carry

    lax.fori_loop(2, HIGH, send_rest, 0)

    table_copy.wait()

    def turn(i, carry):
        flat[i] = raw[i].T
        return carry

    lax.fori_loop(0, flat.shape[0], turn, 0, unroll=2)
    pltpu.make_async_copy(far, far, far_recv).wait()
    chosen_copy = pltpu.make_async_copy(far, chosen, chosen_sem)
    chosen_copy.start()
    chosen_copy.wait()

    lane = gx * 16

    def pairs(level, work):
        slot = order[level]
        first = slot * 16
        at = lane + slot * 2
        for start in range(0, len(work), BATCH):
            done = []
            for (gx_, gy_), (px_, py_) in work[start:start + BATCH]:
                own, cross = chosen[gx_, gy_, 0, at], chosen[gx_, gy_, 0, at + 1]
                own_p, cross_p = chosen[px_, py_, 0, at], chosen[px_, py_, 0, at + 1]
                g, p = gx_ * MIDDLE + gy_, px_ * MIDDLE + py_
                weights = jnp.concatenate([
                    jnp.concatenate([flat[first + own], flat[first + cross_p]], axis=1),
                    jnp.concatenate([flat[first + cross], flat[first + own_p]], axis=1),
                ], axis=0)
                both = jnp.dot(
                    jnp.concatenate([field[g], field[p]], axis=1), weights,
                    preferred_element_type=jnp.float32,
                ).astype(jnp.bfloat16)
                done.append((g, p, both))
            for g, p, both in done:
                field[g] = both[:, :128]
                field[p] = both[:, 128:]

    def arrived(s, carry):
        x = lax.rem(gx - s + HIGH, HIGH)
        group = field.at[pl.ds(x * MIDDLE, MIDDLE)]
        pltpu.make_async_copy(group, group, field_recv.at[s]).wait()
        for level in range(5):
            half = 1 << level
            pairs(level, [((x, y), (x, y + half)) for y in range(MIDDLE) if not y & half])
        return carry

    lax.fori_loop(0, HIGH, arrived, 0)

    def send_back(r):
        y = rotated(gy, r)

        def send(s, carry):
            x = lax.rem(gx + s, HIGH)
            pltpu.make_async_remote_copy(
                field.at[x * MIDDLE + y], out.at[mine], out_send, out_recv,
                device_id=(x, y), device_id_type=MESH,
            ).start()
            return carry

        return send

    def finish(r):
        y = rotated(gy, r)
        for level in range(5, 8):
            half = 1 << (level - 5)
            pairs(level, [((x, y), (x + half, y)) for x in range(HIGH) if not x & half])

    finish(0)

    def later(r, carry):
        finish(r)

        @pl.when(r == 1)
        def _():
            pltpu.make_async_copy(field.at[here], out.at[mine], out_recv).start()
            lax.fori_loop(1, HIGH, send_back(0), 0)

        @pl.when(r > 1)
        def _():
            lax.fori_loop(0, HIGH, send_back(r - 1), 0)

        return carry

    lax.fori_loop(1, MIDDLE, later, 0)
    lax.fori_loop(0, HIGH, send_back(MIDDLE - 1), 0)

    def drain(ref, sem):
        pltpu.make_async_copy(ref, ref, sem).wait()

    drain(near.at[pl.ds(0, MIDDLE - 1)], near_send)
    drain(far.at[pl.ds(0, HIGH - 1)], far_send)
    drain(field.at[pl.ds(0, DEVICES - 1)], field_send)
    drain(field.at[pl.ds(0, DEVICES - 1)], out_send)
    drain(field, out_recv)


def body(vectors, coupling_table, factor_index, level_order):
    hbm, smem = pl.BlockSpec(memory_space=pl.ANY), pl.BlockSpec(memory_space=pltpu.SMEM)
    rank = vectors.shape[-1]
    dma = pltpu.SemaphoreType.DMA
    return pl.pallas_call(
        kernel,
        out_shape=jax.ShapeDtypeStruct(vectors.shape, vectors.dtype),
        in_specs=[smem, hbm, hbm, hbm],
        out_specs=hbm,
        scratch_shapes=[
            pltpu.VMEM(vectors.shape, jnp.bfloat16),
            pltpu.VMEM((128, rank, rank), jnp.bfloat16),
            pltpu.VMEM((128, rank, rank), jnp.bfloat16),
            pltpu.VMEM((MIDDLE, 1, 128), jnp.int32),
            pltpu.VMEM((HIGH, MIDDLE, 1, 128), jnp.int32),
            pltpu.SMEM((HIGH, MIDDLE, 1, 128), jnp.int32),
            dma, dma, dma, dma, dma, dma, dma, dma, dma, dma((HIGH,)),
        ],
        compiler_params=pltpu.CompilerParams(
            collective_id=0, has_side_effects=True, vmem_limit_bytes=32 << 20
        ),
    )(level_order, factor_index.reshape(MIDDLE, 1, 128), vectors, coupling_table.reshape(128, rank, rank))


def solution(mesh):
    placed = (P(("gx", "gy"), None, None), P(), P(("gx", "gy"), None, None), P())
    return jax.shard_map(
        body, mesh=mesh, in_specs=placed, out_specs=P(("gx", "gy"), None, None), check_vma=False
    )
```

```python
import jax
import jax.numpy as jnp
from jax import lax
from jax.experimental import pallas as pl
from jax.experimental.pallas import tpu as pltpu
from jax.sharding import PartitionSpec as P

MESH = pl.DeviceIdType.MESH
HIGH, MIDDLE = 8, 32
DEVICES = HIGH * MIDDLE
BATCH = 4


def rotated(coordinate, step):
    z, y, core = coordinate // 8, lax.rem(coordinate // 2, 4), lax.rem(coordinate, 2)
    return (
        lax.rem(z + lax.rem(step, 4), 4) * 8
        + lax.rem(y + lax.rem(step // 4, 4), 4) * 2
        + lax.rem(core + step // 16, 2)
    )


def kernel(
    order, index, vectors, table, out,
    field, raw, flat, near, far, chosen,
    table_sem, near_send, near_recv, far_send, far_recv, chosen_sem,
    out_send, out_recv, field_send, field_recv, row_in,
):
    gx, gy = lax.axis_index("gx"), lax.axis_index("gy")
    mine = gy * HIGH + gx
    here = gx * MIDDLE + gy

    table_copy = pltpu.make_async_copy(table, raw, table_sem)
    table_copy.start()

    barrier = pltpu.get_barrier_semaphore()

    def greet_row(i, carry):
        to = (gx, lax.rem(gy + i, MIDDLE))
        pl.semaphore_signal(barrier, inc=1, device_id=to, device_id_type=MESH)
        return carry

    def greet_column(i, carry):
        to = (lax.rem(gx + i, HIGH), gy)
        pl.semaphore_signal(barrier, inc=1, device_id=to, device_id_type=MESH)
        return carry

    def row_is_in(i, carry):
        to = (lax.rem(gx + i, HIGH), gy)
        pl.semaphore_signal(row_in.at[gx], inc=1, device_id=to, device_id_type=MESH)
        return carry

    lax.fori_loop(1, MIDDLE, greet_row, 0)
    lax.fori_loop(1, HIGH, greet_column, 0)
    pl.semaphore_wait(barrier, MIDDLE + HIGH - 2)
    lax.fori_loop(1, HIGH, row_is_in, 0)

    def send_index(r, carry):
        to = rotated(gy, r)
        pltpu.make_async_remote_copy(
            index.at[to], near.at[gy], near_send, near_recv, device_id=(gx, to), device_id_type=MESH
        ).start()
        return carry

    z, y, core = gy // 8, lax.rem(gy // 2, 4), lax.rem(gy, 2)
    z_to = [lax.rem(z + i, 4) * 8 for i in range(4)]
    y_to = [lax.rem(y + i, 4) * 2 for i in range(4)]

    def send_group(s, half, skip=0):
        to_x = lax.rem(gx + s, HIGH)
        for i in range(skip, 16):
            to_y = z_to[i % 4] + y_to[i // 4] + half
            pltpu.make_async_remote_copy(
                vectors.at[to_y * HIGH + to_x], field.at[here], field_send, field_recv.at[s],
                device_id=(to_x, to_y), device_id_type=MESH,
            ).start()

    own_index = pltpu.make_async_copy(index.at[gy], near.at[gy], near_recv)
    own_index.start()
    lax.fori_loop(1, MIDDLE, send_index, 0)
    pltpu.make_async_copy(vectors.at[mine], field.at[here], field_recv.at[0]).start()
    send_group(0, 0, 1)

    @pl.when(core == 1)
    def _():
        to = z_to[0] + y_to[0]
        pltpu.make_async_remote_copy(
            vectors.at[to * HIGH + gx], field.at[here], field_send, field_recv.at[0],
            device_id=(gx, to), device_id_type=MESH,
        ).start()

    pl.semaphore_wait(row_in.at[lax.rem(gx + 1, HIGH)], 1)
    send_group(1, 0)
    pltpu.make_async_copy(index, near, near_recv).wait()

    def send_far(s, carry):
        to = lax.rem(gx + s, HIGH)
        pltpu.make_async_remote_copy(
            near, far.at[gx], far_send, far_recv, device_id=(to, gy), device_id_type=MESH
        ).start()
        return carry

    lax.fori_loop(1, HIGH, send_far, 0)
    pltpu.make_async_copy(near, far.at[gx], far_recv).start()

    def send_rest(s, carry):
        pl.semaphore_wait(row_in.at[lax.rem(gx + s, HIGH)], 1)
        send_group(s, 0)
        return carry

    lax.fori_loop(2, HIGH, send_rest, 0)

    send_group(0, 1, 1)

    @pl.when(core == 0)
    def _():
        to = z_to[0] + y_to[0] + 1
        pltpu.make_async_remote_copy(
            vectors.at[to * HIGH + gx], field.at[here], field_send, field_recv.at[0],
            device_id=(gx, to), device_id_type=MESH,
        ).start()

    def send_second(s, carry):
        send_group(s, 1)
        return carry

    lax.fori_loop(1, HIGH, send_second, 0)

    table_copy.wait()

    def turn(i, carry):
        flat[i] = raw[i].T
        return carry

    lax.fori_loop(0, flat.shape[0], turn, 0, unroll=2)
    pltpu.make_async_copy(far, far, far_recv).wait()
    chosen_copy = pltpu.make_async_copy(far, chosen, chosen_sem)
    chosen_copy.start()
    chosen_copy.wait()

    lane = gx * 16

    def pairs(level, work):
        slot = order[level]
        first = slot * 16
        at = lane + slot * 2
        for start in range(0, len(work), BATCH):
            done = []
            for (gx_, gy_), (px_, py_) in work[start:start + BATCH]:
                own, cross = chosen[gx_, gy_, 0, at], chosen[gx_, gy_, 0, at + 1]
                own_p, cross_p = chosen[px_, py_, 0, at], chosen[px_, py_, 0, at + 1]
                g, p = gx_ * MIDDLE + gy_, px_ * MIDDLE + py_
                weights = jnp.concatenate([
                    jnp.concatenate([flat[first + own], flat[first + cross_p]], axis=1),
                    jnp.concatenate([flat[first + cross], flat[first + own_p]], axis=1),
                ], axis=0)
                both = jnp.dot(
                    jnp.concatenate([field[g], field[p]], axis=1), weights,
                    preferred_element_type=jnp.float32,
                ).astype(jnp.bfloat16)
                done.append((g, p, both))
            for g, p, both in done:
                field[g] = both[:, :128]
                field[p] = both[:, 128:]

    def arrived(s, carry):
        x = lax.rem(gx - s + HIGH, HIGH)
        group = field.at[pl.ds(x * MIDDLE, MIDDLE)]
        pltpu.make_async_copy(group, group, field_recv.at[s]).wait()
        for level in range(5):
            half = 1 << level
            pairs(level, [((x, y), (x, y + half)) for y in range(MIDDLE) if not y & half])
        return carry

    lax.fori_loop(0, HIGH, arrived, 0)

    def send_back(r):
        y = rotated(gy, r)

        def send(s, carry):
            x = lax.rem(gx + s, HIGH)
            pltpu.make_async_remote_copy(
                field.at[x * MIDDLE + y], out.at[mine], out_send, out_recv,
                device_id=(x, y), device_id_type=MESH,
            ).start()
            return carry

        return send

    def finish(r):
        y = rotated(gy, r)
        for level in range(5, 8):
            half = 1 << (level - 5)
            pairs(level, [((x, y), (x + half, y)) for x in range(HIGH) if not x & half])

    finish(0)

    def later(r, carry):
        finish(r)

        @pl.when(r == 1)
        def _():
            pltpu.make_async_copy(field.at[here], out.at[mine], out_recv).start()
            lax.fori_loop(1, HIGH, send_back(0), 0)

        @pl.when(r > 1)
        def _():
            lax.fori_loop(0, HIGH, send_back(r - 1), 0)

        return carry

    lax.fori_loop(1, MIDDLE, later, 0)
    lax.fori_loop(0, HIGH, send_back(MIDDLE - 1), 0)

    def drain(ref, sem):
        pltpu.make_async_copy(ref, ref, sem).wait()

    drain(near.at[pl.ds(0, MIDDLE - 1)], near_send)
    drain(far.at[pl.ds(0, HIGH - 1)], far_send)
    drain(field.at[pl.ds(0, DEVICES - 1)], field_send)
    drain(field.at[pl.ds(0, DEVICES - 1)], out_send)
    drain(field, out_recv)


def body(vectors, coupling_table, factor_index, level_order):
    hbm, smem = pl.BlockSpec(memory_space=pltpu.HBM), pl.BlockSpec(memory_space=pltpu.SMEM)
    rank = vectors.shape[-1]
    dma = pltpu.SemaphoreType.DMA
    return pl.pallas_call(
        kernel,
        out_shape=jax.ShapeDtypeStruct(vectors.shape, vectors.dtype),
        in_specs=[smem, pl.BlockSpec(memory_space=pl.ANY), hbm, hbm],
        out_specs=pl.BlockSpec(memory_space=pl.ANY),
        scratch_shapes=[
            pltpu.VMEM(vectors.shape, jnp.bfloat16),
            pltpu.VMEM((128, rank, rank), jnp.bfloat16),
            pltpu.VMEM((128, rank, rank), jnp.bfloat16),
            pltpu.VMEM((MIDDLE, 1, 128), jnp.int32),
            pltpu.VMEM((HIGH, MIDDLE, 1, 128), jnp.int32),
            pltpu.SMEM((HIGH, MIDDLE, 1, 128), jnp.int32),
            dma, dma, dma, dma, dma, dma, dma, dma, dma, dma((HIGH,)),
            pltpu.SemaphoreType.REGULAR((HIGH,)),
        ],
        compiler_params=pltpu.CompilerParams(
            collective_id=0, has_side_effects=True, vmem_limit_bytes=32 << 20
        ),
    )(level_order, factor_index.reshape(MIDDLE, 1, 128), vectors, coupling_table.reshape(128, rank, rank))


def solution(mesh):
    placed = (P(("gx", "gy"), None, None), P(), P(("gx", "gy"), None, None), P())
    return jax.shard_map(
        body, mesh=mesh, in_specs=placed, out_specs=P(("gx", "gy"), None, None), check_vma=False
    )
```

```python
import jax
import jax.numpy as jnp
from jax import lax
from jax.experimental import pallas as pl
from jax.experimental.pallas import tpu as pltpu
from jax.sharding import PartitionSpec as P

MESH = pl.DeviceIdType.MESH
RING, PLANE = 8, 32
DEVICES = RING * PLANE
BATCH = 4
STEPS = (1, 7, 2, 6, 3, 5, 4, 0)


def step_of(k):
    odd = lax.rem(k, 2)
    return (1 - odd) * (k // 2 + 1) + odd * (8 - (k + 1) // 2 - 4 * (k // 7))


def device(z, q):
    return lax.rem(z, 2) * 4 + q // 8, (z // 2) * 8 + lax.rem(q, 8)


def kernel(
    order, index, vectors, table, out,
    field, raw, flat, near, far, chosen,
    table_sem, near_send, near_recv, far_send, far_recv, chosen_sem,
    out_send, out_recv, field_send, field_recv, plane_in,
):
    gx, gy = lax.axis_index("gx"), lax.axis_index("gy")
    x, y, core = lax.rem(gx, 4), lax.rem(gy // 2, 4), lax.rem(gy, 2)
    z = (gy // 8) * 2 + gx // 4
    q = x * 8 + y * 2 + core
    here = z * PLANE + q

    table_copy = pltpu.make_async_copy(table, raw, table_sem)
    table_copy.start()

    z_to = [lax.rem(z + i, RING) for i in range(RING)]
    x_to = [lax.rem(x + i, 4) for i in range(4)]
    y_to = [lax.rem(y + i, 4) for i in range(4)]
    core_to = [core, 1 - core]

    barrier = pltpu.get_barrier_semaphore()

    def greet(at_z, at_q):
        pl.semaphore_signal(barrier, inc=1, device_id=device(at_z, at_q), device_id_type=MESH)

    for k in STEPS[:-1]:
        greet(z_to[k], q)
    for i in range(1, PLANE):
        greet(z, x_to[i % 4] * 8 + y_to[i // 4 % 4] * 2 + core_to[i // 16])
    pl.semaphore_wait(barrier, RING + PLANE - 2)
    for k in STEPS[:-1]:
        pl.semaphore_signal(
            plane_in.at[z], inc=1, device_id=device(z_to[k], q), device_id_type=MESH
        )

    pltpu.make_async_copy(index.at[z], near.at[z], near_recv).start()
    for k in STEPS[:-1]:
        pltpu.make_async_remote_copy(
            index.at[z_to[k]], near.at[z], near_send, near_recv,
            device_id=device(z_to[k], q), device_id_type=MESH,
        ).start()

    def send_group(k, half):
        at_z = z_to[STEPS[k]]
        for i in range(16):
            if STEPS[k] or i:
                at_q = x_to[i % 4] * 8 + y_to[i // 4] * 2 + half
                pltpu.make_async_remote_copy(
                    vectors.at[at_z * PLANE + at_q], field.at[here], field_send, field_recv.at[k],
                    device_id=device(at_z, at_q), device_id_type=MESH,
                ).start()
        if not STEPS[k]:
            @pl.when(core == 1 - half)
            def _():
                at_q = x * 8 + y * 2 + half
                pltpu.make_async_remote_copy(
                    vectors.at[z * PLANE + at_q], field.at[here], field_send, field_recv.at[k],
                    device_id=device(z, at_q), device_id_type=MESH,
                ).start()

    for k in range(RING):
        if STEPS[k]:
            pl.semaphore_wait(plane_in.at[z_to[STEPS[k]]], 1)
        send_group(k, 0)
        if k == 1:
            pltpu.make_async_copy(near, near, near_recv).wait()
            pltpu.make_async_copy(near.at[:, q // 8], far.at[q], far_recv).start()
            for i in range(1, PLANE):
                at_q = x_to[i % 4] * 8 + y_to[i // 4 % 4] * 2 + core_to[i // 16]
                pltpu.make_async_remote_copy(
                    near.at[:, at_q // 8], far.at[q], far_send, far_recv,
                    device_id=device(z, at_q), device_id_type=MESH,
                ).start()
    pltpu.make_async_copy(vectors.at[here], field.at[here], field_recv.at[RING - 1]).start()
    for k in range(RING):
        send_group(k, 1)

    table_copy.wait()

    def turn(i, carry):
        flat[i] = raw[i].T
        return carry

    lax.fori_loop(0, flat.shape[0], turn, 0, unroll=2)
    pltpu.make_async_copy(far, far, far_recv).wait()
    chosen_copy = pltpu.make_async_copy(far, chosen, chosen_sem)
    chosen_copy.start()
    chosen_copy.wait()

    lane = lax.rem(q, 8) * 16

    def pairs(level, work):
        slot = order[level]
        first = slot * 16
        at = lane + slot * 2
        for start in range(0, len(work), BATCH):
            done = []
            for (gz, gq), (pz, pq) in work[start:start + BATCH]:
                own, cross = chosen[gq, gz, 0, at], chosen[gq, gz, 0, at + 1]
                own_p, cross_p = chosen[pq, pz, 0, at], chosen[pq, pz, 0, at + 1]
                g, p = gz * PLANE + gq, pz * PLANE + pq
                weights = jnp.concatenate([
                    jnp.concatenate([flat[first + own], flat[first + cross_p]], axis=1),
                    jnp.concatenate([flat[first + cross], flat[first + own_p]], axis=1),
                ], axis=0)
                both = jnp.dot(
                    jnp.concatenate([field[g], field[p]], axis=1), weights,
                    preferred_element_type=jnp.float32,
                ).astype(jnp.bfloat16)
                done.append((g, p, both))
            for g, p, both in done:
                field[g] = both[:, :128]
                field[p] = both[:, 128:]

    def arrived(k, carry):
        at_z = lax.rem(z - step_of(k) + RING, RING)
        group = field.at[pl.ds(at_z * PLANE, PLANE)]
        pltpu.make_async_copy(group, group, field_recv.at[k]).wait()
        for level in range(3):
            half = 1 << level
            pairs(level, [((at_z, i), (at_z, i + half)) for i in range(PLANE) if not i & half])
        return carry

    lax.fori_loop(0, RING, arrived, 0)

    def place(r):
        return lax.rem(y + lax.rem(r, 4), 4) * 2 + lax.rem(core + r // 4, 2)

    def finish(r):
        yc = place(r)
        for level, dz, dx in ((3, 2, 0), (4, 4, 0), (5, 0, 1), (6, 0, 2), (7, 1, 0)):
            pairs(level, [
                ((i, j * 8 + yc), (i + dz, (j + dx) * 8 + yc))
                for j in range(4) for i in range(RING) if not (i & dz or j & dx)
            ])

    def send_back(r, skip=0):
        yc = place(r)
        for i in range(skip, 32):
            at_z, at_q = z_to[(0, *STEPS)[i % 8]], x_to[i // 8] * 8 + yc
            pltpu.make_async_remote_copy(
                field.at[at_z * PLANE + at_q], out.at[here], out_send, out_recv,
                device_id=device(at_z, at_q), device_id_type=MESH,
            ).start()

    finish(0)

    def later(r, carry):
        finish(r)

        @pl.when(r == 1)
        def _():
            pltpu.make_async_copy(field.at[here], out.at[here], out_recv).start()
            send_back(0, 1)

        @pl.when(r > 1)
        def _():
            send_back(r - 1)

        return carry

    lax.fori_loop(1, 8, later, 0)
    send_back(7)

    def drain(ref, sem):
        pltpu.make_async_copy(ref, ref, sem).wait()

    drain(near.at[pl.ds(0, RING - 1)], near_send)
    drain(far.at[pl.ds(0, PLANE - 1)], far_send)
    drain(field.at[pl.ds(0, DEVICES - 1)], field_send)
    drain(field.at[pl.ds(0, DEVICES - 1)], out_send)
    drain(field, out_recv)


def body(vectors, coupling_table, factor_index, level_order):
    any_space = pl.BlockSpec(memory_space=pl.ANY)
    rank = vectors.shape[-1]
    dma = pltpu.SemaphoreType.DMA
    return pl.pallas_call(
        kernel,
        out_shape=jax.ShapeDtypeStruct(vectors.shape, vectors.dtype),
        in_specs=[pl.BlockSpec(memory_space=pltpu.SMEM), any_space, any_space, any_space],
        out_specs=any_space,
        scratch_shapes=[
            pltpu.VMEM(vectors.shape, jnp.bfloat16),
            pltpu.VMEM((128, rank, rank), jnp.bfloat16),
            pltpu.VMEM((128, rank, rank), jnp.bfloat16),
            pltpu.VMEM((RING, 4, 1, 128), jnp.int32),
            pltpu.VMEM((PLANE, RING, 1, 128), jnp.int32),
            pltpu.SMEM((PLANE, RING, 1, 128), jnp.int32),
            dma, dma, dma, dma, dma, dma, dma, dma, dma, dma((RING,)),
            pltpu.SemaphoreType.REGULAR((RING,)),
        ],
        compiler_params=pltpu.CompilerParams(
            collective_id=0, has_side_effects=True, vmem_limit_bytes=VMEM_LIMIT
        ),
    )(level_order, factor_index.reshape(RING, 4, 1, 128), vectors, coupling_table.reshape(128, rank, rank))


VMEM_LIMIT = 67043328 - (14 << 20)


def solution(mesh):
    placed = (P(("gx", "gy"), None, None), P(), P(("gx", "gy"), None, None), P())
    return jax.shard_map(
        body, mesh=mesh, in_specs=placed, out_specs=P(("gx", "gy"), None, None), check_vma=False
    )
```

```python
import jax
import jax.numpy as jnp
from jax import lax
from jax.experimental import pallas as pl
from jax.experimental.pallas import tpu as pltpu
from jax.sharding import PartitionSpec as P

MESH = pl.DeviceIdType.MESH
RING, PLANE = 8, 32
DEVICES = RING * PLANE
BATCH = 4
STEPS = (1, 7, 2, 6, 3, 5, 4, 0)


def step_of(k):
    odd = lax.rem(k, 2)
    return (1 - odd) * (k // 2 + 1) + odd * (8 - (k + 1) // 2 - 4 * (k // 7))


def device(z, q):
    return lax.rem(z, 2) * 4 + q // 8, (z // 2) * 8 + lax.rem(q, 8)


def kernel(
    order, index, vectors, table, out,
    field, raw, flat, raw_index, stacked, turned, rows, near, far, chosen,
    table_sem, index_sem, near_send, near_recv, far_send, far_recv, chosen_sem,
    out_send, out_recv, field_send, field_recv, plane_in,
):
    gx, gy = lax.axis_index("gx"), lax.axis_index("gy")
    x, y, core = lax.rem(gx, 4), lax.rem(gy // 2, 4), lax.rem(gy, 2)
    z = (gy // 8) * 2 + gx // 4
    q = x * 8 + y * 2 + core
    here = z * PLANE + q

    table_copy = pltpu.make_async_copy(table, raw, table_sem)
    table_copy.start()
    index_copy = pltpu.make_async_copy(index, raw_index, index_sem)
    index_copy.start()

    z_to = [lax.rem(z + i, RING) for i in range(RING)]
    x_to = [lax.rem(x + i, 4) for i in range(4)]
    y_to = [lax.rem(y + i, 4) for i in range(4)]
    core_to = [core, 1 - core]

    barrier = pltpu.get_barrier_semaphore()

    def greet(at_z, at_q):
        pl.semaphore_signal(barrier, inc=1, device_id=device(at_z, at_q), device_id_type=MESH)

    for k in STEPS[:-1]:
        greet(z_to[k], q)
    for i in range(1, PLANE):
        greet(z, x_to[i % 4] * 8 + y_to[i // 4 % 4] * 2 + core_to[i // 16])

    stacked[...] = jnp.zeros_like(stacked)
    index_copy.wait()
    for k in range(8):
        stacked[pl.ds(2 * k, 2), :] = raw_index[k]
    turned[...] = stacked[...].T
    packed = turned[pl.ds(0, PLANE, stride=8), :]
    for e in range(1, 8):
        packed += pltpu.roll(turned[pl.ds(e, PLANE, stride=8), :], 16 * e, 1)
    for i in range(PLANE):
        rows[i // 4, i % 4] = packed[i:i + 1, :]

    pl.semaphore_wait(barrier, RING + PLANE - 2)
    for k in STEPS[:-1]:
        pl.semaphore_signal(
            plane_in.at[z], inc=1, device_id=device(z_to[k], q), device_id_type=MESH
        )

    pltpu.make_async_copy(rows.at[z], near.at[z], near_recv).start()
    for k in STEPS[:-1]:
        pltpu.make_async_remote_copy(
            rows.at[z_to[k]], near.at[z], near_send, near_recv,
            device_id=device(z_to[k], q), device_id_type=MESH,
        ).start()

    def send_one(k, at_q):
        at_z = z_to[STEPS[k]]
        pltpu.make_async_remote_copy(
            vectors.at[at_z * PLANE + at_q], field.at[here], field_send, field_recv.at[k],
            device_id=device(at_z, at_q), device_id_type=MESH,
        ).start()

    def send_group(k, half):
        @pl.when(core == 1 - half)
        def _():
            send_one(k, x * 8 + y * 2 + half)

        for i in range(1, 16):
            send_one(k, x_to[i % 4] * 8 + y_to[i // 4] * 2 + half)

    for k in range(RING - 1):
        send_one(k, q)

    for k in range(RING):
        if STEPS[k]:
            pl.semaphore_wait(plane_in.at[z_to[STEPS[k]]], 1)
        send_group(k, 0)
        if k == 1:
            pltpu.make_async_copy(near, near, near_recv).wait()
            pltpu.make_async_copy(near.at[:, q // 8], far.at[q], far_recv).start()
            for i in range(1, PLANE):
                at_q = x_to[i % 4] * 8 + y_to[i // 4 % 4] * 2 + core_to[i // 16]
                pltpu.make_async_remote_copy(
                    near.at[:, at_q // 8], far.at[q], far_send, far_recv,
                    device_id=device(z, at_q), device_id_type=MESH,
                ).start()
    pltpu.make_async_copy(vectors.at[here], field.at[here], field_recv.at[RING - 1]).start()
    for k in range(RING):
        send_group(k, 1)

    table_copy.wait()

    def turn(i, carry):
        flat[i] = raw[i].T
        return carry

    lax.fori_loop(0, flat.shape[0], turn, 0, unroll=2)
    pltpu.make_async_copy(far, far, far_recv).wait()
    chosen_copy = pltpu.make_async_copy(far, chosen, chosen_sem)
    chosen_copy.start()
    chosen_copy.wait()

    lane = lax.rem(q, 8) * 16

    def pairs(level, work):
        slot = order[level]
        first = slot * 16
        at = lane + slot * 2
        for start in range(0, len(work), BATCH):
            done = []
            for (gz, gq), (pz, pq) in work[start:start + BATCH]:
                own, cross = chosen[gq, gz, 0, at], chosen[gq, gz, 0, at + 1]
                own_p, cross_p = chosen[pq, pz, 0, at], chosen[pq, pz, 0, at + 1]
                g, p = gz * PLANE + gq, pz * PLANE + pq
                weights = jnp.concatenate([
                    jnp.concatenate([flat[first + own], flat[first + cross_p]], axis=1),
                    jnp.concatenate([flat[first + cross], flat[first + own_p]], axis=1),
                ], axis=0)
                both = jnp.dot(
                    jnp.concatenate([field[g], field[p]], axis=1), weights,
                    preferred_element_type=jnp.float32,
                ).astype(jnp.bfloat16)
                done.append((g, p, both))
            for g, p, both in done:
                field[g] = both[:, :128]
                field[p] = both[:, 128:]

    def arrived(k, carry):
        at_z = lax.rem(z - step_of(k) + RING, RING)
        group = field.at[pl.ds(at_z * PLANE, PLANE)]
        pltpu.make_async_copy(group, group, field_recv.at[k]).wait()
        for level in range(3):
            half = 1 << level
            pairs(level, [((at_z, i), (at_z, i + half)) for i in range(PLANE) if not i & half])
        return carry

    lax.fori_loop(0, RING, arrived, 0)

    def place(r):
        return lax.rem(y + lax.rem(r, 4), 4) * 2 + lax.rem(core + r // 4, 2)

    def finish(r):
        yc = place(r)
        for level, dz, dx in ((3, 2, 0), (4, 4, 0), (5, 0, 1), (6, 0, 2), (7, 1, 0)):
            pairs(level, [
                ((i, j * 8 + yc), (i + dz, (j + dx) * 8 + yc))
                for j in range(4) for i in range(RING) if not (i & dz or j & dx)
            ])

    def send_back(r, skip=0):
        yc = place(r)
        for i in range(32 - skip):
            at_z, at_q = z_to[STEPS[6 - i // 4]], x_to[3 - i % 4] * 8 + yc
            pltpu.make_async_remote_copy(
                field.at[at_z * PLANE + at_q], out.at[here], out_send, out_recv,
                device_id=device(at_z, at_q), device_id_type=MESH,
            ).start()

    finish(0)

    def later(r, carry):
        finish(r)

        @pl.when(r == 1)
        def _():
            pltpu.make_async_copy(field.at[here], out.at[here], out_recv).start()
            send_back(0, 1)

        @pl.when(r > 1)
        def _():
            send_back(r - 1)

        return carry

    lax.fori_loop(1, 8, later, 0)
    send_back(7)

    def drain(ref, sem):
        pltpu.make_async_copy(ref, ref, sem).wait()

    drain(near.at[pl.ds(0, RING - 1)], near_send)
    drain(far.at[pl.ds(0, PLANE - 1)], far_send)
    drain(field.at[pl.ds(0, DEVICES - 1)], field_send)
    drain(field.at[pl.ds(0, DEVICES - 1)], out_send)
    drain(field, out_recv)


def body(vectors, coupling_table, factor_index, level_order):
    any_space = pl.BlockSpec(memory_space=pl.ANY)
    rank = vectors.shape[-1]
    dma = pltpu.SemaphoreType.DMA
    return pl.pallas_call(
        kernel,
        out_shape=jax.ShapeDtypeStruct(vectors.shape, vectors.dtype),
        in_specs=[pl.BlockSpec(memory_space=pltpu.SMEM), any_space, any_space, any_space],
        out_specs=any_space,
        scratch_shapes=[
            pltpu.VMEM(vectors.shape, jnp.bfloat16),
            pltpu.VMEM((128, rank, rank), jnp.bfloat16),
            pltpu.VMEM((128, rank, rank), jnp.bfloat16),
            pltpu.VMEM((8, 2, DEVICES), jnp.int32),
            pltpu.VMEM((128, DEVICES), jnp.int32),
            pltpu.VMEM((DEVICES, 128), jnp.int32),
            pltpu.VMEM((RING, 4, 1, 128), jnp.int32),
            pltpu.VMEM((RING, 4, 1, 128), jnp.int32),
            pltpu.VMEM((PLANE, RING, 1, 128), jnp.int32),
            pltpu.SMEM((PLANE, RING, 1, 128), jnp.int32),
            dma, dma, dma, dma, dma, dma, dma, dma, dma, dma, dma((RING,)),
            pltpu.SemaphoreType.REGULAR((RING,)),
        ],
        compiler_params=pltpu.CompilerParams(
            collective_id=0, has_side_effects=True, vmem_limit_bytes=VMEM_LIMIT
        ),
    )(level_order, jnp.transpose(factor_index, (1, 2, 0)), vectors, coupling_table.reshape(128, rank, rank))


VMEM_LIMIT = 67043328 - (14 << 20)


def solution(mesh):
    placed = (P(("gx", "gy"), None, None), P(), P(("gx", "gy"), None, None), P())
    return jax.shard_map(
        body, mesh=mesh, in_specs=placed, out_specs=P(("gx", "gy"), None, None), check_vma=False
    )
```
